512 devices in a mesh: dp: 64 (over z_lo, y, x), seq: 8 (over z_hi, core).
Axes of the slice: x: 4, y: 8, z: 8 (z_hi: 4, z_lo: 2; z = z_hi * 2 + z_lo), core: 2. Of those that a mesh axis runs over, the one named last changes fastest.
Arguments:
- queries: bfloat16 [65536, 4096], P(('dp', 'seq')), may hold values from -48 to 48
- keys: bfloat16 [65536, 1024], P(('dp', 'seq')), may hold values from -6 to 6
- values: bfloat16 [65536, 1024], P(('dp', 'seq')), may hold values from -6 to 6
- out_grad: bfloat16 [65536, 4096], P(('dp', 'seq')), may hold values from -6 to 6
- normed: bfloat16 [65536, 4096], P(('dp', 'seq')), may hold values from -24 to 24
Outputs:
- query_grad: bfloat16 [65536, 4096], P(('dp', 'seq'))
- key_weight_grad: float32 [4096, 1024], P('dp', 'seq')
- value_weight_grad: float32 [4096, 1024], P('dp', 'seq')
The draws below stay inside these ranges and needn't reach their ends.
All inputs are finite; a program needn't handle non-finite values.
Results may differ from the reference program's by a relative error of at most 0.0055.
Values may be sent and summed in bfloat16 or wider, within the bound.
A program may use at most 128 MiB of HBM per device.

```python
import math
import jax
import jax.numpy as jnp
from jax import lax

D = 4096
QH = 32
KV = 8
HD = 128
SEQ_LEN = 1024
TOKENS = 65536


def shared_keys(key):
    base = jax.random.fold_in(key, 11)
    drawn = jax.random.truncated_normal(base, -6.0, 6.0, (TOKENS, KV * HD), jnp.float32)
    return drawn


def draw_keys(key, part):
    return shared_keys(key).astype(jnp.bfloat16)


def draw_queries(key, part):
    base = jax.random.fold_in(key, 23)
    drawn = jax.random.truncated_normal(base, -6.0, 6.0, (TOKENS, QH * HD), jnp.float32)
    return drawn.astype(jnp.bfloat16)


def with_spikes(array, stream_key, source, target, shards_of, factor):
    owner, partner = [(jnp.arange(array.shape[axis_at]) // (array.shape[axis_at] // shards_of)).reshape([-1 if axis == axis_at else 1 for axis in range(array.ndim)]) for axis_at in (source, target)]
    chosen = jax.random.permutation(stream_key, shards_of)[partner]
    strong = (owner == chosen) | (owner == (partner + shards_of // 2) % shards_of)
    return jnp.where(strong, factor * array, array)


def block_levels(stream_key, dims, split, smallest, high):
    factor_of = 1.0
    for dim, blocks in split:
        heights = jax.random.uniform(jax.random.fold_in(jax.random.fold_in(stream_key, 6), dim), (blocks,), jnp.float32, smallest / len(split), high / len(split))
        factor_of = factor_of * jnp.repeat(jnp.exp(heights), dims[dim] // blocks).reshape((-1,) + (1,) * (len(dims) - 1 - dim))
    return factor_of


def bell_draw(own_key, shape, spread, bound, cuts=(), dtype=jnp.bfloat16):
    level = block_levels(own_key, shape, cuts, -0.22, 0.18) if cuts else 1.0
    values = jax.random.normal(own_key, shape, jnp.float32) * spread * level
    return jnp.minimum(jnp.maximum(values, -bound), bound).astype(dtype)


def bell_draw_with(own_key, extent, deviation, limit, split, heavy, held_as=jnp.bfloat16):
    result = deviation * jax.random.normal(own_key, extent, jnp.float32)
    if split:
        result = result * block_levels(own_key, extent, split, -0.22, 0.18)
    return jnp.clip(with_spikes(result, jax.random.fold_in(own_key, 3), *heavy), -limit, limit).astype(held_as)


def setup_inputs(seed: int = 0) -> dict:
    seeds = jax.random.split(jax.random.key(seed), 6)
    queries = draw_queries(jax.random.fold_in(seeds[5], 71), 0)
    keys = draw_keys(jax.random.fold_in(seeds[5], 71), 0)
    values = bell_draw(seeds[2], (TOKENS, KV * HD), 1.0, 6.0, ((0, 512),))
    out_grad = bell_draw(seeds[3], (TOKENS, QH * HD), 1.0, 6.0, ((0, 512),))
    normed = bell_draw_with(seeds[4], (TOKENS, D), 1.0, 24.0, ((0, 512),), (0, 1, 512, 6.0))
    return {"queries": queries, "keys": keys, "values": values, "out_grad": out_grad, "normed": normed}


def unrotate(grad, position):
    half = HD // 2
    freqs = jnp.exp(-math.log(500000.0) * (2.0 * jnp.arange(half).astype(jnp.float32) / HD))
    angle = position.astype(jnp.float32)[:, None] * freqs[None, :]
    cosine = jnp.cos(angle)[:, None, :]
    sine = jnp.sin(angle)[:, None, :]
    first = grad[..., :half]
    second = grad[..., half:]
    return jnp.concatenate([first * cosine + second * sine, second * cosine - first * sine], axis=-1)

def one_sequence(carry, items):
    query_rows, key_rows, value_rows, grad_rows, normed_rows = items
    groups = QH // KV
    scale = 1.0 / math.sqrt(HD)
    qh = query_rows.reshape(SEQ_LEN, QH, HD).astype(jnp.float32)
    kh = jnp.repeat(key_rows.reshape(SEQ_LEN, KV, HD), groups, axis=1).astype(jnp.float32)
    vh = jnp.repeat(value_rows.reshape(SEQ_LEN, KV, HD), groups, axis=1).astype(jnp.float32)
    gh = grad_rows.reshape(SEQ_LEN, QH, HD).astype(jnp.float32)
    scores = jnp.einsum('qhd,khd->hqk', qh, kh) * scale
    position = jnp.arange(SEQ_LEN)
    allowed = position[None, :] <= position[:, None]
    scores = jnp.where(allowed[None], scores, -jnp.inf)
    top = lax.optimization_barrier(jnp.max(scores, axis=-1, keepdims=True))
    expo = jnp.where(allowed[None], jnp.exp(scores - top), 0.0)
    probs = expo / lax.optimization_barrier(jnp.sum(expo, axis=-1, keepdims=True))
    probs_b = lax.optimization_barrier(probs.astype(jnp.bfloat16)).astype(jnp.float32)
    value_heads = jnp.einsum('hqk,qhd->khd', probs_b, gh)
    value_grad = value_heads.reshape(SEQ_LEN, KV, groups, HD).sum(axis=2).reshape(SEQ_LEN, KV * HD).astype(jnp.bfloat16)
    prob_grad = jnp.einsum('qhd,khd->hqk', gh, vh)
    delta = lax.optimization_barrier(jnp.sum(probs * prob_grad, axis=-1, keepdims=True))
    score_grad = lax.optimization_barrier((probs * (prob_grad - delta) * scale).astype(jnp.bfloat16)).astype(jnp.float32)
    query_grad = jnp.einsum('hqk,khd->qhd', score_grad, kh).reshape(SEQ_LEN, QH * HD).astype(jnp.bfloat16)
    key_heads = jnp.einsum('hqk,qhd->khd', score_grad, qh)
    key_sum = key_heads.reshape(SEQ_LEN, KV, groups, HD).sum(axis=2)
    key_grad = unrotate(key_sum, position).reshape(SEQ_LEN, KV * HD).astype(jnp.bfloat16)
    key_total = carry[0] + jnp.dot(normed_rows.T, key_grad, preferred_element_type=jnp.float32)
    value_total = carry[1] + jnp.dot(normed_rows.T, value_grad, preferred_element_type=jnp.float32)
    return ((key_total, value_total), query_grad)

def reference(queries, keys, values, out_grad, normed):
    count = TOKENS // SEQ_LEN
    items = (queries.reshape(count, SEQ_LEN, QH * HD), keys.reshape(count, SEQ_LEN, KV * HD), values.reshape(count, SEQ_LEN, KV * HD), out_grad.reshape(count, SEQ_LEN, QH * HD), normed.reshape(count, SEQ_LEN, D))
    start = (jnp.zeros((D, KV * HD), jnp.float32), jnp.zeros((D, KV * HD), jnp.float32))
    totals, query_grad = lax.scan(one_sequence, start, items)
    return (query_grad.reshape(TOKENS, QH * HD), totals[0], totals[1])
```

```python
import functools
import math

import jax
import jax.numpy as jnp
import numpy as np
from jax import lax
from jax.experimental import pallas as pl
from jax.experimental.pallas import tpu as pltpu
from jax.sharding import PartitionSpec as P

HD = 128
BLOCK = 256


def rotary_tables(length):
    half = HD // 2
    freqs = np.exp(-math.log(500000.0) * (2.0 * np.arange(half, dtype=np.float32) / HD)).astype(np.float32)
    angle = np.arange(length, dtype=np.float32)[:, None] * freqs[None, :]
    cosine, sine = np.cos(angle), np.sin(angle)
    return (
        np.concatenate([cosine, cosine], axis=1).astype(np.float32),
        np.concatenate([sine, -sine], axis=1).astype(np.float32),
    )


def attention_kernel(q_ref, k_ref, v_ref, g_ref, cos_ref, sin_ref, dq_ref, dkv_ref, dk_acc, dv_acc):
    length = q_ref.shape[0]
    heads = q_ref.shape[1] // HD
    scale = 1.0 / math.sqrt(HD)
    rate = scale * math.log2(math.e)
    dk_acc[...] = jnp.zeros_like(dk_acc)
    dv_acc[...] = jnp.zeros_like(dv_acc)
    for first in range(0, length, BLOCK):
        last = first + BLOCK
        rows = pl.ds(first, BLOCK)

        def step(head, carry, first=first, last=last, rows=rows):
            cols = pl.ds(pl.multiple_of(head * HD, HD), HD)
            q = q_ref[rows, cols]
            g = g_ref[rows, cols]
            k = k_ref[:last, :]
            v = v_ref[:last, :]
            contract_last = (((1,), (1,)), ((), ()))
            s = lax.dot_general(k, q, contract_last, preferred_element_type=jnp.float32)
            key_pos = lax.broadcasted_iota(jnp.int32, s.shape, 0)
            query_pos = lax.broadcasted_iota(jnp.int32, s.shape, 1) + first
            s = jnp.where(key_pos <= query_pos, s, -jnp.inf)
            top = jnp.max(s, axis=0, keepdims=True)
            e = jnp.exp2((s - top) * rate)
            p = e * (1.0 / jnp.sum(e, axis=0, keepdims=True))
            dv_acc[:last, :] += jnp.dot(p.astype(jnp.bfloat16), g, preferred_element_type=jnp.float32)
            dp = lax.dot_general(v, g, contract_last, preferred_element_type=jnp.float32)
            delta = jnp.sum(p * dp, axis=0, keepdims=True)
            ds = (p * ((dp - delta) * scale)).astype(jnp.bfloat16)
            dk_acc[:last, :] += jnp.dot(ds, q, preferred_element_type=jnp.float32)
            dq_ref[rows, cols] = lax.dot_general(
                ds, k, (((0,), (0,)), ((), ())), preferred_element_type=jnp.float32
            ).astype(jnp.bfloat16)
            return carry

        lax.fori_loop(0, heads, step, 0)
    dk = dk_acc[...]
    dk = dk * cos_ref[...] + pltpu.roll(dk, HD // 2, 1) * sin_ref[...]
    dkv_ref[:, :HD] = dk.astype(jnp.bfloat16)
    dkv_ref[:, HD:] = dv_acc[...].astype(jnp.bfloat16)


def attention(q, k, v, g):
    length = q.shape[0]
    cosine, sine = rotary_tables(length)
    vmem = pl.BlockSpec(memory_space=pltpu.VMEM)
    return pl.pallas_call(
        attention_kernel,
        out_shape=(
            jax.ShapeDtypeStruct(q.shape, jnp.bfloat16),
            jax.ShapeDtypeStruct((length, 2 * HD), jnp.bfloat16),
        ),
        in_specs=[vmem] * 6,
        out_specs=(vmem, vmem),
        scratch_shapes=[
            pltpu.VMEM((length, HD), jnp.float32),
            pltpu.VMEM((length, HD), jnp.float32),
        ],
        cost_estimate=pl.CostEstimate(flops=4_000_000_000, bytes_accessed=6_000_000, transcendentals=3_000_000),
        name="attention",
    )(q, k, v, g, jnp.asarray(cosine), jnp.asarray(sine))


def local(queries, keys, values, out_grad, normed):
    q, k, v, g = (
        lax.all_to_all(x, "seq", split_axis=1, concat_axis=0, tiled=True)
        for x in (queries, keys, values, out_grad)
    )
    dq, dkv = attention(q, k, v, g)
    query_grad = lax.all_to_all(dq, "seq", split_axis=0, concat_axis=1, tiled=True)
    gathered = lax.all_gather(normed, "seq", axis=0, tiled=True)
    part = lax.dot_general(
        gathered, dkv, (((0,), (0,)), ((), ())), preferred_element_type=jnp.float32
    ).astype(jnp.bfloat16)
    groups = lax.axis_size("dp")
    parts = lax.all_to_all(
        part.reshape(groups, part.shape[0] // groups, 2 * HD), "dp", split_axis=0, concat_axis=0
    )
    total = jnp.sum(parts.astype(jnp.float32), axis=0)
    return (query_grad, total[:, :HD], total[:, HD:])


def solution(mesh):
    rows = P(("dp", "seq"), None)
    return jax.shard_map(
        local,
        mesh=mesh,
        in_specs=(rows,) * 5,
        out_specs=(rows, P("dp", "seq"), P("dp", "seq")),
        check_vma=False,
    )
```

```python
import math

import jax
import jax.numpy as jnp
import numpy as np
from jax import lax
from jax.experimental import pallas as pl
from jax.experimental.pallas import tpu as pltpu
from jax.sharding import PartitionSpec as P

HD = 128
BLOCK = 256


def rotary_tables(length):
    half = HD // 2
    freqs = np.exp(-math.log(500000.0) * (2.0 * np.arange(half, dtype=np.float32) / HD)).astype(np.float32)
    angle = np.arange(length, dtype=np.float32)[:, None] * freqs[None, :]
    cosine, sine = np.cos(angle), np.sin(angle)
    return (
        np.concatenate([cosine, cosine], axis=1).astype(np.float32),
        np.concatenate([sine, -sine], axis=1).astype(np.float32),
    )


BF16 = jnp.bfloat16
F32 = jnp.float32
CHUNKS = 4
GROUP = 8
XS, YS, ZS = 4, 8, 2
MESH = pl.DeviceIdType.MESH


def remote(src, dst, send_sem, recv_sem, device):
    return pltpu.make_async_remote_copy(
        src_ref=src, dst_ref=dst, send_sem=send_sem, recv_sem=recv_sem, device_id=device, device_id_type=MESH
    )


def aligned(index, size):
    return pl.ds(pl.multiple_of(index * size, size), size)


def attend(first, hq, hk, hv, hg, dq, dk_acc, dv_acc, heads):
    scale = 1.0 / math.sqrt(HD)
    rate = scale * math.log2(math.e)
    last = first + BLOCK
    rows = pl.ds(first, BLOCK)
    contract_last = (((1,), (1,)), ((), ()))

    def step(head, carry):
        cols = aligned(head, HD)
        q = hq[rows, cols]
        g = hg[rows, cols]
        k = hk[:last, :]
        v = hv[:last, :]
        s = lax.dot_general(k, q, contract_last, preferred_element_type=F32)
        key_pos = lax.broadcasted_iota(jnp.int32, s.shape, 0)
        query_pos = lax.broadcasted_iota(jnp.int32, s.shape, 1) + first
        s = jnp.where(key_pos <= query_pos, s, -jnp.inf)
        top = jnp.max(s, axis=0, keepdims=True)
        e = jnp.exp2((s - top) * rate)
        p = e * (1.0 / jnp.sum(e, axis=0, keepdims=True))
        dv_acc[:last, :] += jnp.dot(p.astype(BF16), g, preferred_element_type=F32)
        dp = lax.dot_general(v, g, contract_last, preferred_element_type=F32)
        delta = jnp.sum(p * dp, axis=0, keepdims=True)
        ds = (p * ((dp - delta) * scale)).astype(BF16)
        dk_acc[:last, :] += jnp.dot(ds, q, preferred_element_type=F32)
        dq[rows, cols] = lax.dot_general(
            ds, k, (((0,), (0,)), ((), ())), preferred_element_type=F32
        ).astype(BF16)
        return carry

    lax.fori_loop(0, heads, step, 0)


def layer_kernel(
    q_ref, k_ref, v_ref, g_ref, n_ref, cos_ref, sin_ref,
    dq_out, kw_out, vw_out,
    hq, hk, hv, hg, gathered, dq, dk_acc, dv_acc, dkv, part, xrecv, ysend, yrecv, ztotal, zrecv,
    in_send, in_recv, ag_send, ag_recv, dq_send, dq_recv, x_send, x_recv, y_send, y_recv, z_send, z_recv,
):
    tokens, width = n_ref.shape
    length = hq.shape[0]
    heads = hq.shape[1] // HD
    cols = width // CHUNKS
    seq = lax.axis_index("seq")
    dp = lax.axis_index("dp")
    chip, core = seq // 2, seq % 2
    sib = chip * 2 + (1 - core)
    up_chip, down_chip, far_chip = (chip + 1) % 4, (chip + 3) % 4, (chip + 2) % 4
    up, down, far = up_chip * 2 + core, down_chip * 2 + core, far_chip * 2 + core
    zi, yi, xi = dp // (XS * YS), (dp // XS) % YS, dp % XS
    x_peer = [zi * (XS * YS) + yi * XS + (xi + r) % XS for r in range(XS)]
    y_peer = [zi * (XS * YS) + ((yi + r) % YS) * XS + xi for r in range(YS)]
    z_peer = (1 - zi) * (XS * YS) + yi * XS + xi
    peers = [{"seq": (seq + r) % GROUP} for r in range(1, GROUP)]
    peers += [{"dp": x_peer[r]} for r in range(1, XS)]
    peers += [{"dp": y_peer[r]} for r in range(1, YS)]
    peers += [{"dp": z_peer}]

    barrier = pltpu.get_barrier_semaphore()
    for peer in peers:
        pl.semaphore_signal(barrier, inc=1, device_id=peer, device_id_type=MESH)
    pl.semaphore_wait(barrier, len(peers))

    mine = aligned(seq, tokens)
    pairs = ((k_ref, hk), (v_ref, hv), (q_ref, hq), (g_ref, hg))
    sends = []
    enter = []
    for a, (src, dst) in enumerate(pairs):
        piece = dst.shape[1]
        for r in range(1, GROUP):
            to = (seq + r) % GROUP
            copy = remote(
                src.at[:, aligned(to, piece)], dst.at[mine, :],
                in_send.at[a, r - 1], in_recv.at[a, r - 1], {"seq": to},
            )
            copy.start()
            sends.append(copy)
            source = (seq + GROUP - r) % GROUP
            block = dst.at[aligned(source, tokens), :]
            enter.append(remote(block, block, in_send.at[a, r - 1], in_recv.at[a, r - 1], {"seq": to}))

    half = tokens // 2

    def window(block, ch, part_rows=None):
        if part_rows is None:
            rows = aligned(block, tokens)
        else:
            rows = pl.ds(pl.multiple_of(block * tokens + part_rows * half, half), half)
        return gathered.at[rows, pl.ds(ch * cols, cols)]

    def ag(src, dst, ch, kind, to):
        return remote(src, dst, ag_send.at[ch, kind], ag_recv.at[ch, kind], {"seq": to})

    def ag_start(src, dst, ch, kind, to):
        copy = ag(src, dst, ch, kind, to)
        copy.start()
        sends.append(copy)

    def ag_wait(ref, ch, kind):
        ag(ref, ref, ch, kind, sib).wait_recv()

    def own(ch):
        src = n_ref.at[:, pl.ds(ch * cols, cols)]
        for kind, to in ((1, up), (2, down), (0, sib)):
            ag_start(src, window(seq, ch), ch, kind, to)

    def relay(ch):
        ag_wait(window(down, ch), ch, 1)
        ag_start(window(down, ch, 0), window(down, ch, 0), ch, 5, up)
        ag_wait(window(up, ch), ch, 2)
        ag_start(window(up, ch, 1), window(up, ch, 1), ch, 6, down)
        ag_start(window(down, ch), window(down, ch), ch, 3, sib)
        ag_start(window(up, ch), window(up, ch), ch, 4, sib)

    def relay_far(ch):
        ag_wait(window(far, ch, 0), ch, 5)
        ag_start(window(far, ch, 0), window(far, ch, 0), ch, 7, sib)
        ag_wait(window(far, ch, 1), ch, 6)
        ag_start(window(far, ch, 1), window(far, ch, 1), ch, 8, sib)

    def arrived(ch):
        other = 1 - core
        ag_wait(window(sib, ch), ch, 0)
        ag_wait(window(down_chip * 2 + other, ch), ch, 3)
        ag_wait(window(up_chip * 2 + other, ch), ch, 4)
        ag_wait(window(far_chip * 2 + other, ch, 0), ch, 7)
        ag_wait(window(far_chip * 2 + other, ch, 1), ch, 8)

    own(0)
    own(1)

    for src, dst in pairs:
        dst[mine, :] = src[:, aligned(seq, dst.shape[1])]
    gathered[mine, :] = n_ref[...]
    dk_acc[...] = jnp.zeros_like(dk_acc)
    dv_acc[...] = jnp.zeros_like(dv_acc)
    for copy in enter:
        copy.wait_recv()

    attend(0, hq, hk, hv, hg, dq, dk_acc, dv_acc, heads)
    relay(0)
    own(2)
    attend(BLOCK, hq, hk, hv, hg, dq, dk_acc, dv_acc, heads)
    relay_far(0)
    relay(1)
    own(3)
    attend(2 * BLOCK, hq, hk, hv, hg, dq, dk_acc, dv_acc, heads)
    relay_far(1)
    relay(2)
    attend(3 * BLOCK, hq, hk, hv, hg, dq, dk_acc, dv_acc, heads)
    dk = dk_acc[...]
    dk = dk * cos_ref[...] + pltpu.roll(dk, HD // 2, 1) * sin_ref[...]
    dkv[:, :HD] = dk.astype(BF16)
    dkv[:, HD:] = dv_acc[...].astype(BF16)

    share = width // (XS * YS * ZS)

    def weights(ch):
        def step(i, carry):
            at = pl.multiple_of(ch * cols + i * (XS * share), XS * share)
            block = lax.dot_general(
                gathered[:, pl.ds(at, XS * share)], dkv[...], (((0,), (0,)), ((), ())), preferred_element_type=F32
            ).astype(BF16)
            for x in range(XS):
                part[ch, x, i] = block[x * share : (x + 1) * share]
            return carry

        lax.fori_loop(0, cols // (XS * share), step, 0)

    def x_copy(ch, r):
        return remote(
            part.at[ch, (xi + r) % XS], xrecv.at[ch, r - 1],
            x_send.at[ch, r - 1], x_recv.at[ch, r - 1], {"dp": x_peer[r]},
        )

    def scatter_x(ch):
        for r in range(1, XS):
            copy = x_copy(ch, r)
            copy.start()
            sends.append(copy)

    def reduce_x(ch):
        for r in range(1, XS):
            x_copy(ch, r).wait_recv()
        count = cols // (XS * share)
        per = YS // count

        def step(i, carry):
            total = part[ch, xi, i].astype(F32)
            for r in range(1, XS):
                total += xrecv[ch, r - 1, i].astype(F32)
            ysend[(ch % per) * count + i, ch // per] = total.astype(BF16)
            return carry

        lax.fori_loop(0, count, step, 0)

    arrived(0)
    weights(0)
    relay_far(2)
    relay(3)
    scatter_x(0)
    leave = []
    for r in range(1, GROUP):
        to = (seq + r) % GROUP
        width_q = heads * HD
        copy = remote(
            dq.at[aligned(to, tokens), :], dq_out.at[:, aligned(seq, width_q)],
            dq_send.at[r - 1], dq_recv.at[r - 1], {"seq": to},
        )
        copy.start()
        sends.append(copy)
        source = (seq + GROUP - r) % GROUP
        block = dq_out.at[:, aligned(source, width_q)]
        leave.append(remote(block, block, dq_send.at[r - 1], dq_recv.at[r - 1], {"seq": to}))
    dq_out[:, aligned(seq, heads * HD)] = dq[mine, :]
    arrived(1)
    weights(1)
    relay_far(3)
    scatter_x(1)
    reduce_x(0)
    arrived(2)
    weights(2)
    scatter_x(2)
    reduce_x(1)
    arrived(3)
    weights(3)
    scatter_x(3)
    reduce_x(2)
    reduce_x(3)

    def y_copy(r):
        return remote(
            ysend.at[(yi + r) % YS], yrecv.at[r - 1], y_send.at[r - 1], y_recv.at[r - 1], {"dp": y_peer[r]}
        )

    for r in range(1, YS):
        copy = y_copy(r)
        copy.start()
        sends.append(copy)
    for r in range(1, YS):
        y_copy(r).wait_recv()
    for z in range(ZS):
        total = ysend[yi, z].astype(F32)
        for r in range(1, YS):
            total += yrecv[r - 1, z].astype(F32)
        ztotal[z] = total
    last = remote(ztotal.at[1 - zi], zrecv, z_send, z_recv, {"dp": z_peer})
    last.start()
    sends.append(last)
    for copy in leave:
        copy.wait_recv()
    last.wait_recv()
    total = ztotal[zi] + zrecv[...]
    kw_out[...] = total[:, :HD]
    vw_out[...] = total[:, HD:]
    for copy in sends:
        copy.wait_send()


def local(queries, keys, values, out_grad, normed):
    tokens, width = normed.shape
    length = tokens * GROUP
    columns = queries.shape[1] // GROUP
    cosine, sine = rotary_tables(length)
    vmem = pl.BlockSpec(memory_space=pltpu.VMEM)
    share = width // (XS * YS * ZS)
    count = width // CHUNKS // (XS * share)
    dma = pltpu.SemaphoreType.DMA
    return pl.pallas_call(
        layer_kernel,
        out_shape=(
            jax.ShapeDtypeStruct(queries.shape, BF16),
            jax.ShapeDtypeStruct((share, HD), F32),
            jax.ShapeDtypeStruct((share, HD), F32),
        ),
        in_specs=[vmem] * 7,
        out_specs=(vmem,) * 3,
        scratch_shapes=[
            pltpu.VMEM((length, columns), BF16),
            pltpu.VMEM((length, HD), BF16),
            pltpu.VMEM((length, HD), BF16),
            pltpu.VMEM((length, columns), BF16),
            pltpu.VMEM((length, width), BF16),
            pltpu.VMEM((length, columns), BF16),
            pltpu.VMEM((length, HD), F32),
            pltpu.VMEM((length, HD), F32),
            pltpu.VMEM((length, 2 * HD), BF16),
            pltpu.VMEM((CHUNKS, XS, count, share, 2 * HD), BF16),
            pltpu.VMEM((CHUNKS, XS - 1, count, share, 2 * HD), BF16),
            pltpu.VMEM((YS, ZS, share, 2 * HD), BF16),
            pltpu.VMEM((YS - 1, ZS, share, 2 * HD), BF16),
            pltpu.VMEM((ZS, share, 2 * HD), F32),
            pltpu.VMEM((share, 2 * HD), F32),
            dma((4, GROUP - 1)),
            dma((4, GROUP - 1)),
            dma((CHUNKS, 9)),
            dma((CHUNKS, 9)),
            dma((GROUP - 1,)),
            dma((GROUP - 1,)),
            dma((CHUNKS, XS - 1)),
            dma((CHUNKS, XS - 1)),
            dma((YS - 1,)),
            dma((YS - 1,)),
            dma,
            dma,
        ],
        compiler_params=pltpu.CompilerParams(
            collective_id=0, has_side_effects=True, vmem_limit_bytes=56 * 1024 * 1024
        ),
        name="layer",
    )(queries, keys, values, out_grad, normed, jnp.asarray(cosine), jnp.asarray(sine))


def solution(mesh):
    rows = P(("dp", "seq"), None)
    return jax.shard_map(
        local,
        mesh=mesh,
        in_specs=(rows,) * 5,
        out_specs=(rows, P("dp", "seq"), P("dp", "seq")),
        check_vma=False,
    )
```

```python
import math

import jax
import jax.numpy as jnp
import numpy as np
from jax import lax
from jax.experimental import pallas as pl
from jax.experimental.pallas import tpu as pltpu
from jax.sharding import PartitionSpec as P

HD = 128
BLOCK = 256


def rotary_tables(length):
    half = HD // 2
    freqs = np.exp(-math.log(500000.0) * (2.0 * np.arange(half, dtype=np.float32) / HD)).astype(np.float32)
    angle = np.arange(length, dtype=np.float32)[:, None] * freqs[None, :]
    cosine, sine = np.cos(angle), np.sin(angle)
    return (
        np.concatenate([cosine, cosine], axis=1).astype(np.float32),
        np.concatenate([sine, -sine], axis=1).astype(np.float32),
    )


BF16 = jnp.bfloat16
F32 = jnp.float32
CHUNKS = 8
GROUP = 8
EARLY = 3
XS, YS, ZS = 4, 8, 2
MESH = pl.DeviceIdType.MESH


def remote(src, dst, send_sem, recv_sem, device):
    return pltpu.make_async_remote_copy(
        src_ref=src, dst_ref=dst, send_sem=send_sem, recv_sem=recv_sem, device_id=device, device_id_type=MESH
    )


def aligned(index, size):
    return pl.ds(pl.multiple_of(index * size, size), size)


def attend(first, hq, hk, hv, hg, dq, dk_acc, dv_acc, heads):
    scale = 1.0 / math.sqrt(HD)
    rate = scale * math.log2(math.e)
    last = first + BLOCK
    rows = pl.ds(first, BLOCK)
    contract_last = (((1,), (1,)), ((), ()))

    def step(head, carry):
        cols = aligned(head, HD)
        q = hq[rows, cols]
        g = hg[rows, cols]
        k = hk[:last, :]
        v = hv[:last, :]
        s = lax.dot_general(k, q, contract_last, preferred_element_type=F32)
        key_pos = lax.broadcasted_iota(jnp.int32, s.shape, 0)
        query_pos = lax.broadcasted_iota(jnp.int32, s.shape, 1) + first
        s = jnp.where(key_pos <= query_pos, s, -jnp.inf)
        top = jnp.max(s, axis=0, keepdims=True)
        e = jnp.exp2((s - top) * rate)
        p = e * (1.0 / jnp.sum(e, axis=0, keepdims=True))
        dv_acc[:last, :] += jnp.dot(p.astype(BF16), g, preferred_element_type=F32)
        dp = lax.dot_general(v, g, contract_last, preferred_element_type=F32)
        delta = jnp.sum(p * dp, axis=0, keepdims=True)
        ds = (p * ((dp - delta) * scale)).astype(BF16)
        dk_acc[:last, :] += jnp.dot(ds, q, preferred_element_type=F32)
        dq[rows, cols] = lax.dot_general(
            ds, k, (((0,), (0,)), ((), ())), preferred_element_type=F32
        ).astype(BF16)
        return carry

    lax.fori_loop(0, heads, step, 0)


def layer_kernel(
    q_ref, k_ref, v_ref, g_ref, n_ref, cos_ref, sin_ref,
    dq_out, kw_out, vw_out,
    hq, hk, hv, hg, gathered, dq, dk_acc, dv_acc, dkv, part, xrecv, ysend, yrecv, ztotal, zrecv,
    in_send, in_recv, ag_send, ag_recv, dq_send, dq_recv, x_send, x_recv, y_send, y_recv, z_send, z_recv,
):
    tokens, width = n_ref.shape
    length = hq.shape[0]
    heads = hq.shape[1] // HD
    cols = width // CHUNKS
    seq = lax.axis_index("seq")
    dp = lax.axis_index("dp")
    chip, core = seq // 2, seq % 2
    sib = chip * 2 + (1 - core)
    up_chip, down_chip, far_chip = (chip + 1) % 4, (chip + 3) % 4, (chip + 2) % 4
    up, down, far = up_chip * 2 + core, down_chip * 2 + core, far_chip * 2 + core
    zi, yi, xi = dp // (XS * YS), (dp // XS) % YS, dp % XS
    x_peer = [zi * (XS * YS) + yi * XS + (xi + r) % XS for r in range(XS)]
    y_peer = [zi * (XS * YS) + ((yi + r) % YS) * XS + xi for r in range(YS)]
    z_peer = (1 - zi) * (XS * YS) + yi * XS + xi
    peers = [{"seq": (seq + r) % GROUP} for r in range(1, GROUP)]
    peers += [{"dp": x_peer[r]} for r in range(1, XS)]
    peers += [{"dp": y_peer[r]} for r in range(1, YS)]
    peers += [{"dp": z_peer}]

    barrier = pltpu.get_barrier_semaphore()
    for peer in peers:
        pl.semaphore_signal(barrier, inc=1, device_id=peer, device_id_type=MESH)
    pl.semaphore_wait(barrier, len(peers))

    mine = aligned(seq, tokens)
    pairs = ((k_ref, hk), (v_ref, hv), (q_ref, hq), (g_ref, hg))
    sends = []
    enter = []
    for a, (src, dst) in enumerate(pairs):
        piece = dst.shape[1]
        for r in range(1, GROUP):
            to = (seq + r) % GROUP
            copy = remote(
                src.at[:, aligned(to, piece)], dst.at[mine, :],
                in_send.at[a, r - 1], in_recv.at[a, r - 1], {"seq": to},
            )
            copy.start()
            sends.append(copy)
            source = (seq + GROUP - r) % GROUP
            block = dst.at[aligned(source, tokens), :]
            enter.append(remote(block, block, in_send.at[a, r - 1], in_recv.at[a, r - 1], {"seq": to}))

    half = tokens // 2

    def window(block, ch, part_rows=None):
        if part_rows is None:
            rows = aligned(block, tokens)
        else:
            rows = pl.ds(pl.multiple_of(block * tokens + part_rows * half, half), half)
        return gathered.at[rows, pl.ds(ch * cols, cols)]

    def ag(src, dst, ch, kind, to):
        return remote(src, dst, ag_send.at[ch, kind], ag_recv.at[ch, kind], {"seq": to})

    def ag_start(src, dst, ch, kind, to):
        copy = ag(src, dst, ch, kind, to)
        copy.start()
        sends.append(copy)

    def ag_wait(ref, ch, kind):
        ag(ref, ref, ch, kind, sib).wait_recv()

    def own(ch):
        src = n_ref.at[:, pl.ds(ch * cols, cols)]
        for kind, to in ((1, up), (2, down), (0, sib)):
            ag_start(src, window(seq, ch), ch, kind, to)

    def relay(ch):
        ag_wait(window(down, ch), ch, 1)
        ag_start(window(down, ch, 0), window(down, ch, 0), ch, 5, up)
        ag_wait(window(up, ch), ch, 2)
        ag_start(window(up, ch, 1), window(up, ch, 1), ch, 6, down)
        ag_start(window(down, ch), window(down, ch), ch, 3, sib)
        ag_start(window(up, ch), window(up, ch), ch, 4, sib)

    def relay_far(ch):
        ag_wait(window(far, ch, 0), ch, 5)
        ag_start(window(far, ch, 0), window(far, ch, 0), ch, 7, sib)
        ag_wait(window(far, ch, 1), ch, 6)
        ag_start(window(far, ch, 1), window(far, ch, 1), ch, 8, sib)

    def arrived(ch):
        other = 1 - core
        ag_wait(window(sib, ch), ch, 0)
        ag_wait(window(down_chip * 2 + other, ch), ch, 3)
        ag_wait(window(up_chip * 2 + other, ch), ch, 4)
        ag_wait(window(far_chip * 2 + other, ch, 0), ch, 7)
        ag_wait(window(far_chip * 2 + other, ch, 1), ch, 8)

    def advance(ch):
        if ch < CHUNKS:
            relay(ch)
        if ch + 2 < CHUNKS:
            own(ch + 2)
        if ch > 0:
            relay_far(ch - 1)

    own(0)
    own(1)

    for src, dst in pairs:
        dst[mine, :] = src[:, aligned(seq, dst.shape[1])]
    gathered[mine, :] = n_ref[...]
    dk_acc[...] = jnp.zeros_like(dk_acc)
    dv_acc[...] = jnp.zeros_like(dv_acc)
    for copy in enter:
        copy.wait_recv()

    for number, first in enumerate(range(0, length, BLOCK)):
        attend(first, hq, hk, hv, hg, dq, dk_acc, dv_acc, heads)
        if number < EARLY:
            advance(number)
    dk = dk_acc[...]
    dk = dk * cos_ref[...] + pltpu.roll(dk, HD // 2, 1) * sin_ref[...]
    dkv[:, :HD] = dk.astype(BF16)
    dkv[:, HD:] = dv_acc[...].astype(BF16)

    share = width // (XS * YS * ZS)

    def weights(ch):
        def step(i, carry):
            at = pl.multiple_of(ch * cols + i * (XS * share), XS * share)
            block = lax.dot_general(
                gathered[:, pl.ds(at, XS * share)], dkv[...], (((0,), (0,)), ((), ())), preferred_element_type=F32
            ).astype(BF16)
            for x in range(XS):
                part[ch, x, i] = block[x * share : (x + 1) * share]
            return carry

        lax.fori_loop(0, cols // (XS * share), step, 0)

    def x_copy(ch, r):
        return remote(
            part.at[ch, (xi + r) % XS], xrecv.at[ch, r - 1],
            x_send.at[ch, r - 1], x_recv.at[ch, r - 1], {"dp": x_peer[r]},
        )

    def scatter_x(ch):
        for r in range(1, XS):
            copy = x_copy(ch, r)
            copy.start()
            sends.append(copy)

    def reduce_x(ch):
        for r in range(1, XS):
            x_copy(ch, r).wait_recv()
        count = cols // (XS * share)
        per = YS // count

        def step(i, carry):
            total = part[ch, xi, i].astype(F32)
            for r in range(1, XS):
                total += xrecv[ch, r - 1, i].astype(F32)
            ysend[(ch % per) * count + i, ch // per] = total.astype(BF16)
            return carry

        lax.fori_loop(0, count, step, 0)
        for i in range(count):
            target = (ch % per) * count + i

            @pl.when(target != yi)
            def _(target=target):
                y_copy((target + YS - yi) % YS, ch // per, target).start()

    def y_copy(r, z, target):
        return remote(
            ysend.at[target, z], yrecv.at[r - 1, z], y_send.at[r - 1, z], y_recv.at[r - 1, z],
            {"dp": zi * (XS * YS) + target * XS + xi},
        )

    def reduce_y(z):
        for r in range(1, YS):
            y_copy(r, z, (yi + r) % YS).wait_recv()
        total = ysend[yi, z].astype(F32)
        for r in range(1, YS):
            total += yrecv[r - 1, z].astype(F32)
        ztotal[z] = total

    leave = []
    for ch in range(CHUNKS):
        if ch + 1 >= EARLY:
            advance(ch + 1)
        if ch == CHUNKS - 2:
            for r in range(1, GROUP):
                to = (seq + r) % GROUP
                width_q = heads * HD
                copy = remote(
                    dq.at[aligned(to, tokens), :], dq_out.at[:, aligned(seq, width_q)],
                    dq_send.at[r - 1], dq_recv.at[r - 1], {"seq": to},
                )
                copy.start()
                sends.append(copy)
                source = (seq + GROUP - r) % GROUP
                block = dq_out.at[:, aligned(source, width_q)]
                leave.append(remote(block, block, dq_send.at[r - 1], dq_recv.at[r - 1], {"seq": to}))
            dq_out[:, aligned(seq, heads * HD)] = dq[mine, :]
        arrived(ch)
        weights(ch)
        scatter_x(ch)
        if ch > 0:
            reduce_x(ch - 1)
        if ch == CHUNKS - 2:
            reduce_y(0)
    reduce_x(CHUNKS - 1)
    reduce_y(1)
    last = remote(ztotal.at[1 - zi], zrecv, z_send, z_recv, {"dp": z_peer})
    last.start()
    sends.append(last)
    for copy in leave:
        copy.wait_recv()
    last.wait_recv()
    total = ztotal[zi] + zrecv[...]
    kw_out[...] = total[:, :HD]
    vw_out[...] = total[:, HD:]
    for z in range(ZS):
        for r in range(1, YS):
            y_copy(r, z, (yi + r) % YS).wait_send()
    for copy in sends:
        copy.wait_send()


def local(queries, keys, values, out_grad, normed):
    tokens, width = normed.shape
    length = tokens * GROUP
    columns = queries.shape[1] // GROUP
    cosine, sine = rotary_tables(length)
    vmem = pl.BlockSpec(memory_space=pltpu.VMEM)
    share = width // (XS * YS * ZS)
    count = width // CHUNKS // (XS * share)
    dma = pltpu.SemaphoreType.DMA
    return pl.pallas_call(
        layer_kernel,
        out_shape=(
            jax.ShapeDtypeStruct(queries.shape, BF16),
            jax.ShapeDtypeStruct((share, HD), F32),
            jax.ShapeDtypeStruct((share, HD), F32),
        ),
        in_specs=[vmem] * 7,
        out_specs=(vmem,) * 3,
        scratch_shapes=[
            pltpu.VMEM((length, columns), BF16),
            pltpu.VMEM((length, HD), BF16),
            pltpu.VMEM((length, HD), BF16),
            pltpu.VMEM((length, columns), BF16),
            pltpu.VMEM((length, width), BF16),
            pltpu.VMEM((length, columns), BF16),
            pltpu.VMEM((length, HD), F32),
            pltpu.VMEM((length, HD), F32),
            pltpu.VMEM((length, 2 * HD), BF16),
            pltpu.VMEM((CHUNKS, XS, count, share, 2 * HD), BF16),
            pltpu.VMEM((CHUNKS, XS - 1, count, share, 2 * HD), BF16),
            pltpu.VMEM((YS, ZS, share, 2 * HD), BF16),
            pltpu.VMEM((YS - 1, ZS, share, 2 * HD), BF16),
            pltpu.VMEM((ZS, share, 2 * HD), F32),
            pltpu.VMEM((share, 2 * HD), F32),
            dma((4, GROUP - 1)),
            dma((4, GROUP - 1)),
            dma((CHUNKS, 9)),
            dma((CHUNKS, 9)),
            dma((GROUP - 1,)),
            dma((GROUP - 1,)),
            dma((CHUNKS, XS - 1)),
            dma((CHUNKS, XS - 1)),
            dma((YS - 1, ZS)),
            dma((YS - 1, ZS)),
            dma,
            dma,
        ],
        compiler_params=pltpu.CompilerParams(
            collective_id=0, has_side_effects=True, vmem_limit_bytes=56 * 1024 * 1024
        ),
        name="layer",
    )(queries, keys, values, out_grad, normed, jnp.asarray(cosine), jnp.asarray(sine))


def solution(mesh):
    rows = P(("dp", "seq"), None)
    return jax.shard_map(
        local,
        mesh=mesh,
        in_specs=(rows,) * 5,
        out_specs=(rows, P("dp", "seq"), P("dp", "seq")),
        check_vma=False,
    )
```
